32 devices in a mesh: groups: 2 (over y), row: 8 (over z, x), col: 2 (over core).
Axes of the slice: x: 2, y: 2, z: 4, core: 2. Of those that a mesh axis runs over, the one named last changes fastest.
Arguments:
- tokens: bfloat16 [512, 8192], P(('groups', 'col'), 'row'), parts along dimension 0, may hold values from -6 to 6
- w_up: bfloat16 [8192, 32768], P('col', 'row'), may hold values from -0.125 to 0.125
- w_down: bfloat16 [32768, 8192], P('row', 'col'), may hold values from -0.0625 to 0.0625
- mask_up: int32 [64, 256], P(None, 'row'), may hold values 0 or 1
- mask_down: int32 [256, 64], P('row'), may hold values 0 or 1
Outputs:
- mixed: bfloat16 [512, 8192], P(('groups', 'col', 'row')), parts along dimension 0
The draws below stay inside these ranges and needn't reach their ends.
There are 2 independent parts, one for each index of `groups`. The reference program is written for one: setup_inputs(seed, part) draws one part's arguments, and reference() takes and returns one part's arrays. A program takes and returns all parts, laid end to end along the dimension named above; an argument that names none is the same for every part. Nothing has to cross between parts.
All inputs are finite; a program needn't handle non-finite values. No bound on the sum of `mask_up` or of `mask_down` on one device may be relied on, other than what follows from the above.
Results may differ from the reference program's by a relative error of at most 0.005.
Values may be sent and summed in bfloat16 or wider, within the bound.
A program may use at most 512 MiB of HBM per device.

```python
import jax
import jax.numpy as jnp

D = 8192
FF = 32768
BLK = 128
TOKENS = 256
DB = 64
FB = 256


def with_ends(drawn, rng, smallest, largest):
    place = [jax.random.randint(jax.random.fold_in(rng, axis), (), 0, length) for axis, length in enumerate(drawn.shape)]
    longest = drawn.shape.index(max(drawn.shape))
    next_to = place[:longest] + [(place[longest] + 1) % drawn.shape[longest]] + place[longest + 1:]
    return drawn.at[tuple(place)].set(smallest).at[tuple(next_to)].set(largest)


def steps_of(rng, shape, shards, smallest, top_value):
    level = 1.0
    for dim, shards_of in shards:
        heights = jax.random.uniform(jax.random.fold_in(jax.random.fold_in(rng, 6), dim), (shards_of,), jnp.float32, smallest / len(shards), top_value / len(shards))
        level = level * jnp.repeat(jnp.exp(heights), shape[dim] // shards_of).reshape((-1,) + (1,) * (len(shape) - 1 - dim))
    return level


def gaussian(rng, shape, width, limit, split=(), kind=jnp.bfloat16):
    drawn = jax.random.normal(rng, shape, jnp.float32) * width
    if len(split) > 0:
        drawn = steps_of(rng, shape, split, -0.22, 0.18) * drawn
    return jnp.clip(drawn, min=-limit, max=limit).astype(kind)


def setup_inputs(seed: int = 0, part: int = 0) -> dict:
    seeds = jax.random.split(jax.random.key(seed), 6)
    part_keys = jax.random.split(jax.random.fold_in(seeds[5], part), 6)
    return {
        "tokens": gaussian(part_keys[0], (TOKENS, D), 1.0, 6.0, ((0, 2), (1, 8))),
        "w_up": gaussian(seeds[1], (D, FF), (D // 4) ** -0.5, 0.125, ((0, 2), (1, 8))),
        "w_down": gaussian(seeds[2], (FF, D), (FF // 4) ** -0.5, 0.0625, ((0, 8), (1, 2))),
        "mask_up": with_ends((jax.random.randint(seeds[3], (DB, FB), 0, 4) < 1).astype(jnp.int32), jax.random.fold_in(seeds[3], 1), 0, 1),
        "mask_down": with_ends((jax.random.randint(seeds[4], (FB, DB), 0, 4) < 1).astype(jnp.int32), jax.random.fold_in(seeds[4], 1), 0, 1),
    }


def apply_mask(weight, mask):
    rows, cols = weight.shape
    blocks = weight.reshape(mask.shape[0], BLK, mask.shape[1], BLK)
    kept = blocks * mask.astype(weight.dtype)[:, None, :, None]
    return kept.reshape(rows, cols)


def reference(tokens, w_up, w_down, mask_up, mask_down):
    up_masked = apply_mask(w_up, mask_up)
    pre = jnp.dot(tokens, up_masked, preferred_element_type=jnp.float32)
    hidden = jax.nn.gelu(pre, approximate=False).astype(jnp.bfloat16)
    down_masked = apply_mask(w_down, mask_down)
    return jnp.dot(hidden, down_masked, preferred_element_type=jnp.float32).astype(jnp.bfloat16)
```

```python
import jax
import jax.numpy as jnp
from jax import lax
from jax.sharding import PartitionSpec as P


def expand_mask(mask, block, dtype):
    count_r, count_c = mask.shape
    wide = jnp.broadcast_to(mask.astype(dtype)[:, None, :, None], (count_r, block, count_c, block))
    return wide.reshape(count_r * block, count_c * block)


def per_device(tokens, w_up, w_down, mask_up, mask_down):
    cols = lax.axis_size("col")
    block = w_up.shape[0] * cols // mask_up.shape[0]
    core = lax.axis_index("col")
    mine = lax.all_gather(tokens, "row", axis=1, tiled=True)
    x = lax.all_to_all(mine, "col", split_axis=1, concat_axis=0, tiled=True)
    half = mask_up.shape[0] // cols
    mask_u = lax.dynamic_slice_in_dim(mask_up, core * half, half, 0)
    pre = jnp.dot(
        x, w_up * expand_mask(mask_u, block, w_up.dtype), preferred_element_type=jnp.float32
    )
    swap = [(i, (i + 1) % cols) for i in range(cols)]
    pre = pre + lax.ppermute(pre.astype(jnp.bfloat16), "col", swap).astype(jnp.float32)
    hidden = jax.nn.gelu(pre, approximate=False).astype(jnp.bfloat16)
    half_d = mask_down.shape[1] // cols
    mask_d = lax.dynamic_slice_in_dim(mask_down, core * half_d, half_d, 1)
    part = jnp.dot(
        hidden,
        w_down * expand_mask(mask_d, block, w_down.dtype),
        preferred_element_type=jnp.float32,
    )
    part = lax.all_to_all(
        part.astype(jnp.bfloat16), "col", split_axis=0, concat_axis=1, tiled=True
    )
    return lax.psum_scatter(part, "row", scatter_dimension=0, tiled=True).astype(jnp.bfloat16)


def solution(mesh):
    return jax.shard_map(
        per_device,
        mesh=mesh,
        in_specs=(
            P(("groups", "col"), "row"),
            P("col", "row"),
            P("row", "col"),
            P(None, "row"),
            P("row", None),
        ),
        out_specs=P(("groups", "col", "row"), None),
        check_vma=False,
    )
```

```python
import functools

import jax
import jax.numpy as jnp
from jax import lax
from jax.experimental import pallas as pl
from jax.experimental.pallas import tpu as pltpu
from jax.sharding import PartitionSpec as P


def expand_mask(mask, block, dtype):
    count_r, count_c = mask.shape
    wide = jnp.broadcast_to(mask.astype(dtype)[:, None, :, None], (count_r, block, count_c, block))
    return wide.reshape(count_r * block, count_c * block)


def general(tokens, w_up, w_down, mask_up, mask_down):
    cols = lax.axis_size("col")
    block = w_up.shape[0] * cols // mask_up.shape[0]
    core = lax.axis_index("col")
    mine = lax.all_gather(tokens, "row", axis=1, tiled=True)
    x = lax.all_to_all(mine, "col", split_axis=1, concat_axis=0, tiled=True)
    half = mask_up.shape[0] // cols
    mask_u = lax.dynamic_slice_in_dim(mask_up, core * half, half, 0)
    pre = jnp.dot(
        x, w_up * expand_mask(mask_u, block, w_up.dtype), preferred_element_type=jnp.float32
    )
    swap = [(i, (i + 1) % cols) for i in range(cols)]
    pre = pre + lax.ppermute(pre.astype(jnp.bfloat16), "col", swap).astype(jnp.float32)
    hidden = jax.nn.gelu(pre, approximate=False).astype(jnp.bfloat16)
    half_d = mask_down.shape[1] // cols
    mask_d = lax.dynamic_slice_in_dim(mask_down, core * half_d, half_d, 1)
    part = jnp.dot(
        hidden,
        w_down * expand_mask(mask_d, block, w_down.dtype),
        preferred_element_type=jnp.float32,
    )
    part = lax.all_to_all(
        part.astype(jnp.bfloat16), "col", split_axis=0, concat_axis=1, tiled=True
    )
    return lax.psum_scatter(part, "row", scatter_dimension=0, tiled=True).astype(jnp.bfloat16)


MESH = pl.DeviceIdType.MESH
BF16, F32 = jnp.bfloat16, jnp.float32
LAG = 2


def gelu(v):
    return 0.5 * v * (1.0 + lax.erf(v * 0.7071067811865476))


def kernel(
    block,
    tokens, w_up, w_down, mask_up, mask_down,
    out,
    w, x_all, acc, other, hid, part, own, to_x, from_x, to_z, from_left, from_right, final,
    load_sem, w_sem, x_send, x_recv, pre_send, pre_recv, hid_send, hid_recv,
    rs_send, rs_recv, right_send, right_recv, left_send, left_recv, out_sem,
):
    row, core = lax.axis_index("row"), lax.axis_index("col")
    z, x = row // 2, row % 2
    chunks, depth, wide = w.shape
    feats = x_all.shape[-1]
    half = chunks * wide
    count = 8

    def loop(steps, body):
        lax.fori_loop(0, steps, lambda i, _: (body(i), 0)[1], 0)

    def cols(n):
        return pl.ds(pl.multiple_of(n * wide, wide), wide)

    def load_w(source, n):
        return pltpu.make_async_copy(source.at[:, cols(n)], w.at[n], w_sem.at[n])

    loop(chunks, lambda n: load_w(w_up, n).start())
    load = pltpu.make_async_copy(tokens, x_all.at[row, core], load_sem)
    load.start()

    barrier = pltpu.get_barrier_semaphore()
    right, left = {"row": row + 2}, {"row": row - 2}
    across, mate = {"row": z * 2 + 1 - x}, {"col": 1 - core}
    has_right, has_left = z < 3, z > 0

    def greet(device):
        pl.semaphore_signal(barrier, inc=1, device_id=device, device_id_type=MESH)

    greet(across)
    greet(mate)
    pl.when(has_right)(lambda: greet(right))
    pl.when(has_left)(lambda: greet(left))
    ends = jnp.where(has_right, 1, 0) + jnp.where(has_left, 1, 0)
    pl.semaphore_wait(barrier, 2 + ends)
    load.wait()

    def copy_x(kind, r, device, which):
        return pltpu.make_async_remote_copy(
            src_ref=x_all.at[r, which], dst_ref=x_all.at[r, which],
            send_sem=x_send.at[kind, r], recv_sem=x_recv.at[r, which],
            device_id=device, device_id_type=MESH,
        )

    def to_mate(zp, xp):
        @pl.when(zp // 2 == 1 - core)
        def _():
            copy_x(3, zp * 2 + xp, mate, core).start()

    def pass_on(zp, go_right, go_left):
        r = zp * 2 + x
        pl.when(go_right)(lambda: copy_x(0, r, right, core).start())
        pl.when(go_left)(lambda: copy_x(1, r, left, core).start())
        copy_x(2, r, across, core).start()
        to_mate(zp, x)

    def arrive(zp, xp):
        copy_x(2, zp * 2 + xp, across, core).wait_recv()

    pass_on(z, has_right, has_left)

    def step(d):
        if d < 4:

            @pl.when(z - d >= 0)
            def _():
                arrive(z - d, x)
                pass_on(z - d, has_right, False)

            @pl.when(z + d <= 3)
            def _():
                arrive(z + d, x)
                pass_on(z + d, False, has_left)

        @pl.when(z - (d - 1) >= 0)
        def _():
            arrive(z - (d - 1), 1 - x)
            to_mate(z - (d - 1), 1 - x)

        if d > 1:

            @pl.when(z + (d - 1) <= 3)
            def _():
                arrive(z + (d - 1), 1 - x)
                to_mate(z + (d - 1), 1 - x)

    def copy_pre(n):
        return pltpu.make_async_remote_copy(
            src_ref=acc.at[n, 1 - core], dst_ref=other.at[n],
            send_sem=pre_send.at[n], recv_sem=pre_recv.at[n],
            device_id=mate, device_id_type=MESH,
        )

    def masked(n, start, mask, blocks):
        parts = []
        for j in range(blocks):
            keep = mask[pl.ds(start + j, 1), cols(n)].astype(BF16)
            rows = pl.ds(pl.multiple_of((start + j) * block, block), block)
            parts.append(w[n, rows, :] * keep)
        return jnp.concatenate(parts, axis=0)

    def up(r, first, last):
        copy_x(3, r, mate, 1 - core).wait_recv()
        blocks = feats // block
        start = (r - 4 * core) * blocks

        def body(n):
            if first:
                load_w(w_up, n).wait()
            done = jnp.dot(
                x_all[r].reshape(-1, feats), masked(n, start, mask_up, blocks),
                preferred_element_type=F32,
            ).reshape(acc.shape[1:])
            acc[n] = done if first else acc[n] + done
            if last:
                copy_pre(n).start()
                load_w(w_down, n).start()

        loop(chunks, body)

    low = 2 * core
    near = jnp.clip(z, low, low + 1)
    far = 2 * low + 1 - near
    step(1)
    step(2)
    up(near * 2 + x, True, False)
    step(3)
    up(far * 2 + x, False, False)
    up(near * 2 + 1 - x, False, False)
    step(4)
    up(far * 2 + 1 - x, False, True)

    def copy_hid(n, which):
        return pltpu.make_async_remote_copy(
            src_ref=hid.at[n, which], dst_ref=hid.at[n, which],
            send_sem=hid_send.at[n], recv_sem=hid_recv.at[n],
            device_id=mate, device_id_type=MESH,
        )

    def finish(n):
        copy_pre(n).wait_recv()
        hid[n, core] = gelu(acc[n, core] + other[n]).astype(BF16)
        copy_hid(n, core).start()

    loop(chunks, finish)
    loop(chunks, lambda n: copy_hid(n, 1 - core).wait_recv())

    def copy_rs(n):
        return pltpu.make_async_remote_copy(
            src_ref=to_x.at[n], dst_ref=from_x.at[n],
            send_sem=rs_send.at[n], recv_sem=rs_recv.at[n],
            device_id=across, device_id_type=MESH,
        )

    def copy_right(n, zp):
        return pltpu.make_async_remote_copy(
            src_ref=to_z.at[n, zp], dst_ref=from_left.at[n, zp],
            send_sem=right_send.at[n, zp], recv_sem=right_recv.at[n, zp],
            device_id=right, device_id_type=MESH,
        )

    def copy_left(n, zp):
        return pltpu.make_async_remote_copy(
            src_ref=to_z.at[n, zp], dst_ref=from_right.at[n, zp],
            send_sem=left_send.at[n, zp], recv_sem=left_recv.at[n, zp],
            device_id=left, device_id_type=MESH,
        )

    def down(n):
        load_w(w_down, n).wait()
        part[...] = jnp.zeros_like(part)
        blocks = wide // block

        def body(k):
            part[...] += jnp.dot(
                hid[k].reshape(-1, wide), masked(n, k * blocks, mask_down, blocks),
                preferred_element_type=F32,
            ).reshape(part.shape)

        loop(depth // wide, body)
        for zp in range(4):
            for cp in range(2):
                to_x[n, zp, cp] = part[cp, zp, 1 - x].astype(BF16)
        copy_rs(n).start()
        for zp in range(4):
            for cp in range(2):
                own[n, zp, cp] = part[cp, zp, x]

    def take_x(n):
        copy_rs(n).wait_recv()
        own[n] = own[n] + from_x[n].astype(F32)

    def go_right(n):
        for zp in (3, 2, 1, 0):

            @pl.when(has_left & (zp >= z))
            def _():
                copy_right(n, zp).wait_recv()
                own[n, zp] = own[n, zp] + from_left[n, zp].astype(F32)

            @pl.when(zp > z)
            def _():
                to_z[n, zp] = own[n, zp].astype(BF16)
                copy_right(n, zp).start()

    def go_left(n):
        for zp in (0, 1, 2, 3):

            @pl.when(has_right & (zp <= z))
            def _():
                copy_left(n, zp).wait_recv()
                own[n, zp] = own[n, zp] + from_right[n, zp].astype(F32)

            @pl.when(zp < z)
            def _():
                to_z[n, zp] = own[n, zp].astype(BF16)
                copy_left(n, zp).start()

    def pipeline(i):
        for n, stage in (
            (i, down), (i - LAG, take_x), (i - LAG - z, go_right), (i - LAG - 3 + z, go_left),
        ):
            pl.when((n >= 0) & (n < chunks))(functools.partial(stage, n))

    loop(chunks + LAG + 3, pipeline)

    def store(n):
        final[:, cols(n)] = own[n, z, 1 - core].astype(BF16)
        place = pl.ds(pl.multiple_of(core * half + n * wide, wide), wide)
        out[:, place] = own[n, z, core].astype(BF16)

    loop(chunks, store)
    place = pl.ds(pl.multiple_of(core * half, half), half)
    last = pltpu.make_async_remote_copy(
        src_ref=final, dst_ref=out.at[:, place],
        send_sem=out_sem.at[0], recv_sem=out_sem.at[1],
        device_id=mate, device_id_type=MESH,
    )
    last.start()

    for zp in range(4):
        r = zp * 2 + x
        pl.when(has_right & (zp <= z))(lambda r=r: copy_x(0, r, right, core).wait_send())
        pl.when(has_left & (zp >= z))(lambda r=r: copy_x(1, r, left, core).wait_send())
        copy_x(2, r, across, core).wait_send()
        for xp in range(2):

            @pl.when(zp // 2 == 1 - core)
            def _(r=zp * 2 + xp):
                copy_x(3, r, mate, core).wait_send()

    def left_behind(n):
        copy_pre(n).wait_send()
        copy_hid(n, core).wait_send()
        copy_rs(n).wait_send()
        for zp in range(4):
            pl.when(zp > z)(lambda zp=zp: copy_right(n, zp).wait_send())
            pl.when(zp < z)(lambda zp=zp: copy_left(n, zp).wait_send())

    loop(chunks, left_behind)
    last.wait()


def fused(tokens, w_up, w_down, mask_up, mask_down):
    core = lax.axis_index("col")
    block = w_up.shape[0] * 2 // mask_up.shape[0]
    rows_up, cols_down = mask_up.shape[0] // 2, mask_down.shape[1] // 2
    mask_up = lax.dynamic_slice_in_dim(mask_up, core * rows_up, rows_up, 0)
    mask_down = lax.dynamic_slice_in_dim(mask_down, core * cols_down, cols_down, 1)
    mask_up = jnp.repeat(mask_up.astype(F32), block, axis=1)
    mask_down = jnp.repeat(mask_down.astype(F32), block, axis=1)
    count, feats = tokens.shape
    wide, depth = WIDE, w_up.shape[0]
    chunks = w_up.shape[1] // wide
    few = count // 8
    dma = pltpu.SemaphoreType.DMA
    vmem = pl.BlockSpec(memory_space=pltpu.VMEM)
    hbm = pl.BlockSpec(memory_space=pl.ANY)
    travel = (chunks, 4, 2, few, wide)
    return pl.pallas_call(
        functools.partial(kernel, block),
        out_shape=jax.ShapeDtypeStruct((few, w_down.shape[1] * 2), BF16),
        in_specs=[hbm, hbm, hbm, vmem, vmem],
        out_specs=vmem,
        scratch_shapes=[
            pltpu.VMEM((chunks, depth, wide), BF16),
            pltpu.VMEM((8, 2, count, feats), BF16),
            pltpu.VMEM((chunks, 2, count, wide), F32),
            pltpu.VMEM((chunks, count, wide), F32),
            pltpu.VMEM((chunks, 2, count, wide), BF16),
            pltpu.VMEM((2, 4, 2, few, wide), F32),
            pltpu.VMEM(travel, F32),
            pltpu.VMEM(travel, BF16),
            pltpu.VMEM(travel, BF16),
            pltpu.VMEM(travel, BF16),
            pltpu.VMEM(travel, BF16),
            pltpu.VMEM(travel, BF16),
            pltpu.VMEM((few, w_down.shape[1]), BF16),
            dma,
            dma((chunks,)),
            dma((4, 8)),
            dma((8, 2)),
            dma((chunks,)), dma((chunks,)),
            dma((chunks,)), dma((chunks,)),
            dma((chunks,)), dma((chunks,)),
            dma((chunks, 4)), dma((chunks, 4)),
            dma((chunks, 4)), dma((chunks, 4)),
            dma((2,)),
        ],
        compiler_params=pltpu.CompilerParams(
            collective_id=0, has_side_effects=True, vmem_limit_bytes=63 * 2**20
        ),
    )(tokens, w_up, w_down, mask_up, mask_down)


WIDE = 512


def per_device(tokens, w_up, w_down, mask_up, mask_down):
    sizes = (lax.axis_size("row"), lax.axis_size("col"))
    square = w_up.shape[0] == w_up.shape[1] == w_down.shape[0] == w_down.shape[1]
    if sizes == (8, 2) and square and tokens.shape[0] % 128 == 0 and w_up.shape[1] % WIDE == 0:
        return fused(tokens, w_up, w_down, mask_up, mask_down)
    return general(tokens, w_up, w_down, mask_up, mask_down)


def solution(mesh):
    return jax.shard_map(
        per_device,
        mesh=mesh,
        in_specs=(
            P(("groups", "col"), "row"),
            P("col", "row"),
            P("row", "col"),
            P(None, "row"),
            P("row", None),
        ),
        out_specs=P(("groups", "col", "row"), None),
        check_vma=False,
    )
```

```python
import functools

import jax
import jax.numpy as jnp
from jax import lax
from jax.experimental import pallas as pl
from jax.experimental.pallas import tpu as pltpu
from jax.sharding import PartitionSpec as P


def expand_mask(mask, block, dtype):
    count_r, count_c = mask.shape
    wide = jnp.broadcast_to(mask.astype(dtype)[:, None, :, None], (count_r, block, count_c, block))
    return wide.reshape(count_r * block, count_c * block)


def general(tokens, w_up, w_down, mask_up, mask_down):
    cols = lax.axis_size("col")
    block = w_up.shape[0] * cols // mask_up.shape[0]
    core = lax.axis_index("col")
    mine = lax.all_gather(tokens, "row", axis=1, tiled=True)
    x = lax.all_to_all(mine, "col", split_axis=1, concat_axis=0, tiled=True)
    half = mask_up.shape[0] // cols
    mask_u = lax.dynamic_slice_in_dim(mask_up, core * half, half, 0)
    pre = jnp.dot(
        x, w_up * expand_mask(mask_u, block, w_up.dtype), preferred_element_type=jnp.float32
    )
    swap = [(i, (i + 1) % cols) for i in range(cols)]
    pre = pre + lax.ppermute(pre.astype(jnp.bfloat16), "col", swap).astype(jnp.float32)
    hidden = jax.nn.gelu(pre, approximate=False).astype(jnp.bfloat16)
    half_d = mask_down.shape[1] // cols
    mask_d = lax.dynamic_slice_in_dim(mask_down, core * half_d, half_d, 1)
    part = jnp.dot(
        hidden,
        w_down * expand_mask(mask_d, block, w_down.dtype),
        preferred_element_type=jnp.float32,
    )
    part = lax.all_to_all(
        part.astype(jnp.bfloat16), "col", split_axis=0, concat_axis=1, tiled=True
    )
    return lax.psum_scatter(part, "row", scatter_dimension=0, tiled=True).astype(jnp.bfloat16)


MESH = pl.DeviceIdType.MESH
BF16, F32 = jnp.bfloat16, jnp.float32
LAG = 2


def gelu(v):
    return 0.5 * v * (1.0 + lax.erf(v * 0.7071067811865476))


def kernel(
    block,
    tokens, w_up, w_down, mask_up, mask_down,
    out,
    w, x_all, acc, other, hid, part, own, to_x, from_x, to_z, from_left, from_right, final,
    load_sem, w_sem, x_send, x_recv, pre_send, pre_recv, hid_send, hid_recv,
    rs_send, rs_recv, right_send, right_recv, left_send, left_recv, out_sem,
):
    row, core = lax.axis_index("row"), lax.axis_index("col")
    z, x = row // 2, row % 2
    chunks, _, tall, wide = acc.shape
    slots, feats, _ = w.shape
    half = chunks * wide
    ratio = wide // block
    tall = tall // 2

    def loop(steps, body):
        lax.fori_loop(0, steps, lambda i, _: (body(i), 0)[1], 0)

    def cols(n):
        return pl.ds(pl.multiple_of(n * wide, wide), wide)

    def load_w(source, part_of, s, n):
        rows = pl.ds(pl.multiple_of(part_of * feats, feats), feats)
        return pltpu.make_async_copy(
            source.at[rows, cols(n)], w.at[s, :, cols(n)], w_sem.at[s, n]
        )

    def load_up(r, s, n):
        return load_w(w_up, r - slots * core, s, n)

    def load_down(s, n):
        return load_w(w_down, s, s, n)

    load = pltpu.make_async_copy(tokens, x_all.at[row, core], load_sem)
    load.start()

    barrier = pltpu.get_barrier_semaphore()
    right, left = {"row": row + 2}, {"row": row - 2}
    across, mate = {"row": z * 2 + 1 - x}, {"col": 1 - core}
    has_right, has_left = z < 3, z > 0

    def greet(device):
        pl.semaphore_signal(barrier, inc=1, device_id=device, device_id_type=MESH)

    greet(across)
    greet(mate)
    pl.when(has_right)(lambda: greet(right))
    pl.when(has_left)(lambda: greet(left))
    ends = jnp.where(has_right, 1, 0) + jnp.where(has_left, 1, 0)
    pl.semaphore_wait(barrier, 2 + ends)
    load.wait()

    def copy_x(kind, r, device, which, h):
        rows = pl.ds(h * tall, tall)
        return pltpu.make_async_remote_copy(
            src_ref=x_all.at[r, which, rows], dst_ref=x_all.at[r, which, rows],
            send_sem=x_send.at[kind, r, h], recv_sem=x_recv.at[r, which, h],
            device_id=device, device_id_type=MESH,
        )

    def to_mate(zp, xp, h):
        @pl.when(zp // 2 == 1 - core)
        def _():
            copy_x(3, zp * 2 + xp, mate, core, h).start()

    def pass_on(zp, go_right, go_left, h):
        r = zp * 2 + x
        pl.when(go_right)(lambda: copy_x(0, r, right, core, h).start())
        pl.when(go_left)(lambda: copy_x(1, r, left, core, h).start())
        copy_x(2, r, across, core, h).start()
        to_mate(zp, x, h)

    def arrive(zp, xp, h):
        copy_x(2, zp * 2 + xp, across, core, h).wait_recv()

    for h in (0, 1):
        pass_on(z, has_right, has_left, h)

    def step(d):
        for h in (0, 1):
            if d < 4:

                @pl.when(z - d >= 0)
                def _():
                    arrive(z - d, x, h)
                    pass_on(z - d, has_right, False, h)

                @pl.when(z + d <= 3)
                def _():
                    arrive(z + d, x, h)
                    pass_on(z + d, False, has_left, h)

        for h in (0, 1):

            @pl.when(z - (d - 1) >= 0)
            def _():
                arrive(z - (d - 1), 1 - x, h)
                to_mate(z - (d - 1), 1 - x, h)

            if d > 1:

                @pl.when(z + (d - 1) <= 3)
                def _():
                    arrive(z + (d - 1), 1 - x, h)
                    to_mate(z + (d - 1), 1 - x, h)

    def copy_pre(n):
        return pltpu.make_async_remote_copy(
            src_ref=acc.at[n, 1 - core], dst_ref=other.at[n],
            send_sem=pre_send.at[n], recv_sem=pre_recv.at[n],
            device_id=mate, device_id_type=MESH,
        )

    def masked(s, first, n, mask, mask_row, mask_col, blocks):
        parts = []
        for j in range(blocks):
            rows = pl.ds(pl.multiple_of(first + j * block, block), block)
            tiles = []
            for t in range(ratio):
                place = pl.ds(pl.multiple_of(n * wide + t * block, block), block)
                keep = mask[mask_row + j, mask_col + t].astype(F32)
                tiles.append(w[s, rows, place] * jnp.full((block, block), keep, F32).astype(BF16))
            parts.append(jnp.concatenate(tiles, axis=1))
        return jnp.concatenate(parts, axis=0)

    def up(r, s):
        for h in (0, 1):
            copy_x(3, r, mate, 1 - core, h).wait_recv()
        blocks = feats // block

        def body(n):
            load_up(r, s, n).wait()
            done = jnp.dot(
                x_all[r].reshape(-1, feats),
                masked(s, 0, n, mask_up, r * blocks, n * ratio, blocks),
                preferred_element_type=F32,
            ).reshape(acc.shape[1:])
            acc[n] = done if s == 0 else acc[n] + done
            if s == slots - 1:
                copy_pre(n).start()
            load_down(s, n).start()

        loop(chunks, body)

    low = 2 * core
    near = jnp.clip(z, low, low + 1)
    far = 2 * low + 1 - near
    order = (near * 2 + x, far * 2 + x, near * 2 + 1 - x, far * 2 + 1 - x)

    def fetch(s):
        loop(chunks, lambda n: load_up(order[s], s, n).start())

    fetch(0)
    step(1)
    fetch(1)
    step(2)
    fetch(2)
    up(order[0], 0)
    step(3)
    fetch(3)
    up(order[1], 1)
    up(order[2], 2)
    step(4)
    up(order[3], 3)

    def copy_hid(n, which):
        return pltpu.make_async_remote_copy(
            src_ref=hid.at[n, which], dst_ref=hid.at[n, which],
            send_sem=hid_send.at[n], recv_sem=hid_recv.at[n],
            device_id=mate, device_id_type=MESH,
        )

    def finish(n):
        copy_pre(n).wait_recv()
        hid[n, core] = gelu(acc[n, core] + other[n]).astype(BF16)
        copy_hid(n, core).start()

    loop(chunks, finish)
    loop(chunks, lambda n: copy_hid(n, 1 - core).wait_recv())

    def copy_rs(n):
        return pltpu.make_async_remote_copy(
            src_ref=to_x.at[n], dst_ref=from_x.at[n],
            send_sem=rs_send.at[n], recv_sem=rs_recv.at[n],
            device_id=across, device_id_type=MESH,
        )

    def copy_right(n, zp):
        return pltpu.make_async_remote_copy(
            src_ref=to_z.at[n, zp], dst_ref=from_left.at[n, zp],
            send_sem=right_send.at[n, zp], recv_sem=right_recv.at[n, zp],
            device_id=right, device_id_type=MESH,
        )

    def copy_left(n, zp):
        return pltpu.make_async_remote_copy(
            src_ref=to_z.at[n, zp], dst_ref=from_right.at[n, zp],
            send_sem=left_send.at[n, zp], recv_sem=left_recv.at[n, zp],
            device_id=left, device_id_type=MESH,
        )

    def down(n):
        for s in range(slots):
            load_down(s, n).wait()
        part[...] = jnp.zeros_like(part)
        per = feats // wide

        def body(k):
            keep = masked(
                k // per, (k % per) * wide, n, mask_down, k * ratio, (core * chunks + n) * ratio, ratio
            )
            part[...] += jnp.dot(
                hid[k].reshape(-1, wide), keep,
                preferred_element_type=F32,
            ).reshape(part.shape)

        loop(slots * per, body)
        for zp in range(4):
            for cp in range(2):
                to_x[n, zp, cp] = part[cp, zp, 1 - x].astype(BF16)
        copy_rs(n).start()
        for zp in range(4):
            for cp in range(2):
                own[n, zp, cp] = part[cp, zp, x]

    def take_x(n):
        copy_rs(n).wait_recv()
        own[n] = own[n] + from_x[n].astype(F32)

    def go_right(n):
        for zp in (3, 2, 1, 0):

            @pl.when(has_left & (zp >= z))
            def _():
                copy_right(n, zp).wait_recv()
                own[n, zp] = own[n, zp] + from_left[n, zp].astype(F32)

            @pl.when(zp > z)
            def _():
                to_z[n, zp] = own[n, zp].astype(BF16)
                copy_right(n, zp).start()

    def go_left(n):
        for zp in (0, 1, 2, 3):

            @pl.when(has_right & (zp <= z))
            def _():
                copy_left(n, zp).wait_recv()
                own[n, zp] = own[n, zp] + from_right[n, zp].astype(F32)

            @pl.when(zp < z)
            def _():
                to_z[n, zp] = own[n, zp].astype(BF16)
                copy_left(n, zp).start()

    def pipeline(i):
        for n, stage in (
            (i, down), (i - LAG, take_x), (i - LAG - z, go_right), (i - LAG - 3 + z, go_left),
        ):
            pl.when((n >= 0) & (n < chunks))(functools.partial(stage, n))

    loop(chunks + LAG + 3, pipeline)

    def store(n):
        final[:, cols(n)] = own[n, z, 1 - core].astype(BF16)
        place = pl.ds(pl.multiple_of(core * half + n * wide, wide), wide)
        out[:, place] = own[n, z, core].astype(BF16)

    loop(chunks, store)
    place = pl.ds(pl.multiple_of(core * half, half), half)
    last = pltpu.make_async_remote_copy(
        src_ref=final, dst_ref=out.at[:, place],
        send_sem=out_sem.at[0], recv_sem=out_sem.at[1],
        device_id=mate, device_id_type=MESH,
    )
    last.start()

    for h in (0, 1):
        for zp in range(4):
            r = zp * 2 + x
            pl.when(has_right & (zp <= z))(lambda: copy_x(0, r, right, core, h).wait_send())
            pl.when(has_left & (zp >= z))(lambda: copy_x(1, r, left, core, h).wait_send())
            copy_x(2, r, across, core, h).wait_send()
            for xp in range(2):

                @pl.when(zp // 2 == 1 - core)
                def _():
                    copy_x(3, zp * 2 + xp, mate, core, h).wait_send()

    def left_behind(n):
        copy_pre(n).wait_send()
        copy_hid(n, core).wait_send()
        copy_rs(n).wait_send()
        for zp in range(4):
            pl.when(zp > z)(lambda zp=zp: copy_right(n, zp).wait_send())
            pl.when(zp < z)(lambda zp=zp: copy_left(n, zp).wait_send())

    loop(chunks, left_behind)
    last.wait()


def fused(tokens, w_up, w_down, mask_up, mask_down):
    block = w_up.shape[0] * 2 // mask_up.shape[0]
    count, feats = tokens.shape
    wide, depth = WIDE, w_up.shape[0]
    chunks = w_up.shape[1] // wide
    few = count // 8
    dma = pltpu.SemaphoreType.DMA
    vmem = pl.BlockSpec(memory_space=pltpu.VMEM)
    hbm = pl.BlockSpec(memory_space=pl.ANY)
    smem = pl.BlockSpec(memory_space=pltpu.SMEM)
    travel = (chunks, 4, 2, few, wide)
    return pl.pallas_call(
        functools.partial(kernel, block),
        out_shape=jax.ShapeDtypeStruct((few, w_down.shape[1] * 2), BF16),
        in_specs=[hbm, hbm, hbm, smem, smem],
        out_specs=vmem,
        scratch_shapes=[
            pltpu.VMEM((4, depth // 4, w_up.shape[1]), BF16),
            pltpu.VMEM((8, 2, count, feats), BF16),
            pltpu.VMEM((chunks, 2, count, wide), F32),
            pltpu.VMEM((chunks, count, wide), F32),
            pltpu.VMEM((chunks, 2, count, wide), BF16),
            pltpu.VMEM((2, 4, 2, few, wide), F32),
            pltpu.VMEM(travel, F32),
            pltpu.VMEM(travel, BF16),
            pltpu.VMEM(travel, BF16),
            pltpu.VMEM(travel, BF16),
            pltpu.VMEM(travel, BF16),
            pltpu.VMEM(travel, BF16),
            pltpu.VMEM((few, w_down.shape[1]), BF16),
            dma,
            dma((4, chunks)),
            dma((4, 8, 2)),
            dma((8, 2, 2)),
            dma((chunks,)), dma((chunks,)),
            dma((chunks,)), dma((chunks,)),
            dma((chunks,)), dma((chunks,)),
            dma((chunks, 4)), dma((chunks, 4)),
            dma((chunks, 4)), dma((chunks, 4)),
            dma((2,)),
        ],
        compiler_params=pltpu.CompilerParams(
            collective_id=0, has_side_effects=True, vmem_limit_bytes=63 * 2**20
        ),
    )(tokens, w_up, w_down, mask_up, mask_down)


WIDE = 512


def per_device(tokens, w_up, w_down, mask_up, mask_down):
    sizes = (lax.axis_size("row"), lax.axis_size("col"))
    square = tokens.shape[1] * 4 == w_up.shape[0] == w_up.shape[1] == w_down.shape[0] == w_down.shape[1]
    if sizes == (8, 2) and square and tokens.shape[0] % 128 == 0 and w_up.shape[1] % WIDE == 0:
        return fused(tokens, w_up, w_down, mask_up, mask_down)
    return general(tokens, w_up, w_down, mask_up, mask_down)


def solution(mesh):
    return jax.shard_map(
        per_device,
        mesh=mesh,
        in_specs=(
            P(("groups", "col"), "row"),
            P("col", "row"),
            P("row", "col"),
            P(None, "row"),
            P("row", None),
        ),
        out_specs=P(("groups", "col", "row"), None),
        check_vma=False,
    )
```

```python
import functools

import jax
import jax.numpy as jnp
from jax import lax
from jax.experimental import pallas as pl
from jax.experimental.pallas import tpu as pltpu
from jax.sharding import PartitionSpec as P


def expand_mask(mask, block, dtype):
    count_r, count_c = mask.shape
    wide = jnp.broadcast_to(mask.astype(dtype)[:, None, :, None], (count_r, block, count_c, block))
    return wide.reshape(count_r * block, count_c * block)


def general(tokens, w_up, w_down, mask_up, mask_down):
    cols = lax.axis_size("col")
    block = w_up.shape[0] * cols // mask_up.shape[0]
    core = lax.axis_index("col")
    mine = lax.all_gather(tokens, "row", axis=1, tiled=True)
    x = lax.all_to_all(mine, "col", split_axis=1, concat_axis=0, tiled=True)
    half = mask_up.shape[0] // cols
    mask_u = lax.dynamic_slice_in_dim(mask_up, core * half, half, 0)
    pre = jnp.dot(
        x, w_up * expand_mask(mask_u, block, w_up.dtype), preferred_element_type=jnp.float32
    )
    swap = [(i, (i + 1) % cols) for i in range(cols)]
    pre = pre + lax.ppermute(pre.astype(jnp.bfloat16), "col", swap).astype(jnp.float32)
    hidden = jax.nn.gelu(pre, approximate=False).astype(jnp.bfloat16)
    half_d = mask_down.shape[1] // cols
    mask_d = lax.dynamic_slice_in_dim(mask_down, core * half_d, half_d, 1)
    part = jnp.dot(
        hidden,
        w_down * expand_mask(mask_d, block, w_down.dtype),
        preferred_element_type=jnp.float32,
    )
    part = lax.all_to_all(
        part.astype(jnp.bfloat16), "col", split_axis=0, concat_axis=1, tiled=True
    )
    return lax.psum_scatter(part, "row", scatter_dimension=0, tiled=True).astype(jnp.bfloat16)


MESH = pl.DeviceIdType.MESH
BF16, F32 = jnp.bfloat16, jnp.float32
LAG = 1


def gelu(v):
    return 0.5 * v * (1.0 + lax.erf(v * 0.7071067811865476))


def kernel(
    block,
    tokens, w_up, w_down, mask_up, mask_down,
    out,
    w, x_all, acc, other, hid, part, own, to_x, from_x, to_z, from_left, from_right, final,
    load_sem, w_sem, x_send, x_recv, pre_send, pre_recv, hid_send, hid_recv,
    rs_send, rs_recv, right_send, right_recv, left_send, left_recv, out_sem,
):
    row, core = lax.axis_index("row"), lax.axis_index("col")
    z, x = row // 2, row % 2
    chunks, _, tall, wide = acc.shape
    slots, feats, _ = w.shape
    half = chunks * wide
    ratio = wide // block
    tall = tall // 2

    def loop(steps, body):
        lax.fori_loop(0, steps, lambda i, _: (body(i), 0)[1], 0)

    def cols(n):
        return pl.ds(pl.multiple_of(n * wide, wide), wide)

    def load_w(source, part_of, s, n):
        rows = pl.ds(pl.multiple_of(part_of * feats, feats), feats)
        return pltpu.make_async_copy(
            source.at[rows, cols(n)], w.at[s, :, cols(n)], w_sem.at[s, n]
        )

    def load_up(r, s, n):
        return load_w(w_up, r - slots * core, s, n)

    def load_down(s, n):
        return load_w(w_down, s, s, n)

    load = pltpu.make_async_copy(tokens, x_all.at[row, core], load_sem)
    load.start()

    barrier = pltpu.get_barrier_semaphore()
    right, left = {"row": row + 2}, {"row": row - 2}
    across, mate = {"row": z * 2 + 1 - x}, {"col": 1 - core}
    has_right, has_left = z < 3, z > 0

    def greet(device):
        pl.semaphore_signal(barrier, inc=1, device_id=device, device_id_type=MESH)

    greet(across)
    greet(mate)
    pl.when(has_right)(lambda: greet(right))
    pl.when(has_left)(lambda: greet(left))
    ends = jnp.where(has_right, 1, 0) + jnp.where(has_left, 1, 0)
    pl.semaphore_wait(barrier, 2 + ends)
    load.wait()

    def copy_x(kind, r, device, which, h):
        rows = pl.ds(h * tall, tall)
        return pltpu.make_async_remote_copy(
            src_ref=x_all.at[r, which, rows], dst_ref=x_all.at[r, which, rows],
            send_sem=x_send.at[kind, r, h], recv_sem=x_recv.at[r, which, h],
            device_id=device, device_id_type=MESH,
        )

    def to_mate(zp, xp, h):
        @pl.when(zp // 2 == 1 - core)
        def _():
            copy_x(3, zp * 2 + xp, mate, core, h).start()

    def pass_on(zp, go_right, go_left, h):
        r = zp * 2 + x
        pl.when(go_right)(lambda: copy_x(0, r, right, core, h).start())
        pl.when(go_left)(lambda: copy_x(1, r, left, core, h).start())
        copy_x(2, r, across, core, h).start()
        to_mate(zp, x, h)

    def arrive(zp, xp, h):
        copy_x(2, zp * 2 + xp, across, core, h).wait_recv()

    for h in (0, 1):
        pass_on(z, has_right, has_left, h)

    def step(d):
        for h in (0, 1):
            if d < 4:

                @pl.when(z - d >= 0)
                def _():
                    arrive(z - d, x, h)
                    pass_on(z - d, has_right, False, h)

                @pl.when(z + d <= 3)
                def _():
                    arrive(z + d, x, h)
                    pass_on(z + d, False, has_left, h)

        for h in (0, 1):

            @pl.when(z - (d - 1) >= 0)
            def _():
                arrive(z - (d - 1), 1 - x, h)
                to_mate(z - (d - 1), 1 - x, h)

            if d > 1:

                @pl.when(z + (d - 1) <= 3)
                def _():
                    arrive(z + (d - 1), 1 - x, h)
                    to_mate(z + (d - 1), 1 - x, h)

    def copy_pre(n):
        return pltpu.make_async_remote_copy(
            src_ref=acc.at[n, 1 - core], dst_ref=other.at[n],
            send_sem=pre_send.at[n], recv_sem=pre_recv.at[n],
            device_id=mate, device_id_type=MESH,
        )

    def masked(s, first, n, mask, mask_row, mask_col, blocks):
        parts = []
        for j in range(blocks):
            rows = pl.ds(pl.multiple_of(first + j * block, block), block)
            tiles = []
            for t in range(ratio):
                place = pl.ds(pl.multiple_of(n * wide + t * block, block), block)
                keep = mask[mask_row + j, mask_col + t].astype(F32)
                tiles.append(w[s, rows, place] * jnp.full((block, block), keep, F32).astype(BF16))
            parts.append(jnp.concatenate(tiles, axis=1))
        return jnp.concatenate(parts, axis=0)

    def up(r, s):
        for h in (0, 1):
            copy_x(3, r, mate, 1 - core, h).wait_recv()
        blocks = feats // block

        def body(n):
            load_up(r, s, n).wait()
            done = jnp.dot(
                x_all[r].reshape(-1, feats),
                masked(s, 0, n, mask_up, r * blocks, n * ratio, blocks),
                preferred_element_type=F32,
            ).reshape(acc.shape[1:])
            acc[n] = done if s == 0 else acc[n] + done
            if s == slots - 1:
                copy_pre(n).start()
            load_down(s, n).start()

        loop(chunks, body)

    low = 2 * core
    near = jnp.clip(z, low, low + 1)
    far = 2 * low + 1 - near
    order = (near * 2 + x, far * 2 + x, near * 2 + 1 - x, far * 2 + 1 - x)

    def fetch(s):
        loop(chunks, lambda n: load_up(order[s], s, n).start())

    fetch(0)
    step(1)
    fetch(1)
    step(2)
    fetch(2)
    up(order[0], 0)
    step(3)
    fetch(3)
    up(order[1], 1)
    up(order[2], 2)
    step(4)
    up(order[3], 3)

    def copy_hid(n, which):
        return pltpu.make_async_remote_copy(
            src_ref=hid.at[n, which], dst_ref=hid.at[n, which],
            send_sem=hid_send.at[n], recv_sem=hid_recv.at[n],
            device_id=mate, device_id_type=MESH,
        )

    def finish(n):
        copy_pre(n).wait_recv()
        hid[n, core] = gelu(acc[n, core] + other[n]).astype(BF16)
        copy_hid(n, core).start()

    loop(chunks, finish)
    loop(chunks, lambda n: copy_hid(n, 1 - core).wait_recv())

    def copy_rs(n):
        return pltpu.make_async_remote_copy(
            src_ref=to_x.at[n], dst_ref=from_x.at[n],
            send_sem=rs_send.at[n], recv_sem=rs_recv.at[n],
            device_id=across, device_id_type=MESH,
        )

    def copy_right(n, zp):
        return pltpu.make_async_remote_copy(
            src_ref=to_z.at[n, zp], dst_ref=from_left.at[n, zp],
            send_sem=right_send.at[n, zp], recv_sem=right_recv.at[n, zp],
            device_id=right, device_id_type=MESH,
        )

    def copy_left(n, zp):
        return pltpu.make_async_remote_copy(
            src_ref=to_z.at[n, zp], dst_ref=from_right.at[n, zp],
            send_sem=left_send.at[n, zp], recv_sem=left_recv.at[n, zp],
            device_id=left, device_id_type=MESH,
        )

    def down(n):
        for s in range(slots):
            load_down(s, n).wait()
        part[...] = jnp.zeros_like(part)
        per = feats // wide

        def body(k):
            keep = masked(
                k // per, (k % per) * wide, n, mask_down, k * ratio, (core * chunks + n) * ratio, ratio
            )
            part[...] += jnp.dot(
                hid[k].reshape(-1, wide), keep,
                preferred_element_type=F32,
            ).reshape(part.shape)

        loop(slots * per, body)
        for zp in range(4):
            for cp in range(2):
                to_x[n, zp, cp] = part[cp, zp, 1 - x].astype(BF16)
        copy_rs(n).start()
        for zp in range(4):
            for cp in range(2):
                own[n, zp, cp] = part[cp, zp, x]

    def take_x(n):
        copy_rs(n).wait_recv()
        own[n] = own[n] + from_x[n].astype(F32)

    def go_right(n):
        for zp in (3, 2, 1, 0):

            @pl.when(has_left & (zp >= z))
            def _():
                copy_right(n, zp).wait_recv()
                own[n, zp] = own[n, zp] + from_left[n, zp].astype(F32)

            @pl.when(zp > z)
            def _():
                to_z[n, zp] = own[n, zp].astype(BF16)
                copy_right(n, zp).start()

    def go_left(n):
        for zp in (0, 1, 2, 3):

            @pl.when(has_right & (zp <= z))
            def _():
                copy_left(n, zp).wait_recv()
                own[n, zp] = own[n, zp] + from_right[n, zp].astype(F32)

            @pl.when(zp < z)
            def _():
                to_z[n, zp] = own[n, zp].astype(BF16)
                copy_left(n, zp).start()

    def pipeline(i):
        for n, stage in (
            (i, down), (i - LAG, take_x), (i - LAG - z, go_right), (i - LAG - 3 + z, go_left),
        ):
            pl.when((n >= 0) & (n < chunks))(functools.partial(stage, n))

    loop(chunks + LAG + 3, pipeline)

    def store(n):
        final[:, cols(n)] = own[n, z, 1 - core].astype(BF16)
        place = pl.ds(pl.multiple_of(core * half + n * wide, wide), wide)
        out[:, place] = own[n, z, core].astype(BF16)

    loop(chunks, store)
    place = pl.ds(pl.multiple_of(core * half, half), half)
    last = pltpu.make_async_remote_copy(
        src_ref=final, dst_ref=out.at[:, place],
        send_sem=out_sem.at[0], recv_sem=out_sem.at[1],
        device_id=mate, device_id_type=MESH,
    )
    last.start()

    for h in (0, 1):
        for zp in range(4):
            r = zp * 2 + x
            pl.when(has_right & (zp <= z))(lambda: copy_x(0, r, right, core, h).wait_send())
            pl.when(has_left & (zp >= z))(lambda: copy_x(1, r, left, core, h).wait_send())
            copy_x(2, r, across, core, h).wait_send()
            for xp in range(2):

                @pl.when(zp // 2 == 1 - core)
                def _():
                    copy_x(3, zp * 2 + xp, mate, core, h).wait_send()

    def left_behind(n):
        copy_pre(n).wait_send()
        copy_hid(n, core).wait_send()
        copy_rs(n).wait_send()
        for zp in range(4):
            pl.when(zp > z)(lambda zp=zp: copy_right(n, zp).wait_send())
            pl.when(zp < z)(lambda zp=zp: copy_left(n, zp).wait_send())

    loop(chunks, left_behind)
    last.wait()


def fused(tokens, w_up, w_down, mask_up, mask_down):
    block = w_up.shape[0] * 2 // mask_up.shape[0]
    count, feats = tokens.shape
    wide, depth = WIDE, w_up.shape[0]
    chunks = w_up.shape[1] // wide
    few = count // 8
    dma = pltpu.SemaphoreType.DMA
    vmem = pl.BlockSpec(memory_space=pltpu.VMEM)
    hbm = pl.BlockSpec(memory_space=pl.ANY)
    smem = pl.BlockSpec(memory_space=pltpu.SMEM)
    travel = (chunks, 4, 2, few, wide)
    return pl.pallas_call(
        functools.partial(kernel, block),
        out_shape=jax.ShapeDtypeStruct((few, w_down.shape[1] * 2), BF16),
        in_specs=[hbm, hbm, hbm, smem, smem],
        out_specs=vmem,
        scratch_shapes=[
            pltpu.VMEM((4, depth // 4, w_up.shape[1]), BF16),
            pltpu.VMEM((8, 2, count, feats), BF16),
            pltpu.VMEM((chunks, 2, count, wide), F32),
            pltpu.VMEM((chunks, count, wide), F32),
            pltpu.VMEM((chunks, 2, count, wide), BF16),
            pltpu.VMEM((2, 4, 2, few, wide), F32),
            pltpu.VMEM(travel, F32),
            pltpu.VMEM(travel, BF16),
            pltpu.VMEM(travel, BF16),
            pltpu.VMEM(travel, BF16),
            pltpu.VMEM(travel, BF16),
            pltpu.VMEM(travel, BF16),
            pltpu.VMEM((few, w_down.shape[1]), BF16),
            dma,
            dma((4, chunks)),
            dma((4, 8, 2)),
            dma((8, 2, 2)),
            dma((chunks,)), dma((chunks,)),
            dma((chunks,)), dma((chunks,)),
            dma((chunks,)), dma((chunks,)),
            dma((chunks, 4)), dma((chunks, 4)),
            dma((chunks, 4)), dma((chunks, 4)),
            dma((2,)),
        ],
        compiler_params=pltpu.CompilerParams(
            collective_id=0, has_side_effects=True, vmem_limit_bytes=63 * 2**20
        ),
    )(tokens, w_up, w_down, mask_up, mask_down)


WIDE = 512


def per_device(tokens, w_up, w_down, mask_up, mask_down):
    sizes = (lax.axis_size("row"), lax.axis_size("col"))
    square = tokens.shape[1] * 4 == w_up.shape[0] == w_up.shape[1] == w_down.shape[0] == w_down.shape[1]
    if sizes == (8, 2) and square and tokens.shape[0] % 128 == 0 and w_up.shape[1] % WIDE == 0:
        return fused(tokens, w_up, w_down, mask_up, mask_down)
    return general(tokens, w_up, w_down, mask_up, mask_down)


def solution(mesh):
    return jax.shard_map(
        per_device,
        mesh=mesh,
        in_specs=(
            P(("groups", "col"), "row"),
            P("col", "row"),
            P("row", "col"),
            P(None, "row"),
            P("row", None),
        ),
        out_specs=P(("groups", "col", "row"), None),
        check_vma=False,
    )
```
